32 devices in a mesh: strip: 8 (over z, x), lev: 4 (over y, core).
Axes of the slice: x: 2, y: 2, z: 4, core: 2. Of those that a mesh axis runs over, the one named last changes fastest.
Arguments:
- cotangent: float32 [4, 256, 128, 128], P(None, 'lev', 'strip'), may hold values from -6 to 6
- blocks: float32 [4, 256, 64], P(None, 'lev'), may hold values from -0.25 to 1.3
- couple: float32 [4, 4, 128, 128], P(None, 'lev', 'strip'), may hold values from 0 to 1, as said below
- kappa: float32 [128, 128], P('strip'), may hold values from 0.05 to 0.24
Outputs:
- field_adjoint: float32 [4, 256, 128, 128], P(None, 'lev', 'strip')
The draws below stay inside these ranges and needn't reach their ends.
Inputs may be any that keep to these rules, and one draw needn't show every extreme that they name: `couple`: coupling weights lie in 0 to 1.
All inputs are finite; a program needn't handle non-finite values.
Results may differ from the reference program's by a relative error of at most 0.0001.
Values sent between devices are 32-bit elements; how exact they have to be, the bound alone decides.
No kernel may reach another device: no remote copies, remote signals or barrier semaphores. Data moves between devices by JAX's collectives and lax.ppermute only.
A program may use at most 64 MiB of HBM per device.

```python
import jax
import jax.numpy as jnp
from jax import lax

FIELDS = 4
PIECE = 64
NY = 128
LEV = 256
NX = 128


def draw_blocks(key, part):
    segment_parts = LEV // PIECE
    first, second = jax.random.split(key, 2)
    diagonal = jax.random.uniform(first, (4, segment_parts, 1, PIECE), jnp.float32, 0.7, 1.3)
    offdiag = jnp.clip(0.05 * jax.random.normal(second, (4, segment_parts, PIECE, PIECE), jnp.float32), -0.25, 0.25)
    identity = jnp.eye(PIECE, dtype=jnp.float32)
    matrix = offdiag * (1.0 - identity) + identity * diagonal
    return matrix.reshape(4, LEV, PIECE).astype(jnp.float32)


def draw_couple(key, part):
    segment_parts = LEV // PIECE
    key_list = jax.random.split(key, 6)
    share = 0.5
    slowly = jax.random.bernoulli(key_list[0], share, (4, 1, NX, NY))
    spread = jax.random.uniform(key_list[1], (4, 1, NX, NY), jnp.float32, 0.2, 0.8)
    jitter = jax.random.uniform(key_list[2], (4, segment_parts, NX, NY), jnp.float32, 0.985, 1.0)
    slow_rate = jnp.exp(-spread / segment_parts) * jitter
    fast_rate = jax.random.uniform(key_list[3], (4, segment_parts, NX, NY), jnp.float32, 0.1, 0.4)
    pulse_groups = jax.random.bernoulli(key_list[4], 2.0 / segment_parts, (1, segment_parts, 1, 1))
    coupling_magnitude = jax.random.uniform(key_list[5], (1, segment_parts, 1, 1), jnp.float32, 0.5, 0.8)
    multiplier = jnp.where(pulse_groups, coupling_magnitude, 1.0)
    retain = jnp.where(slowly, slow_rate * multiplier, fast_rate)
    return retain.astype(jnp.float32)


def steps_of(key, shape, pieces, least, largest):
    level = 1.0
    for dim, shards_of in pieces:
        steps = jax.random.uniform(jax.random.fold_in(jax.random.fold_in(key, 6), dim), (shards_of,), jnp.float32, least / len(pieces), largest / len(pieces))
        level = level * jnp.repeat(jnp.exp(steps), shape[dim] // shards_of).reshape((-1,) + (1,) * (len(shape) - 1 - dim))
    return level


def gaussian(stream_key, extent, scale, reach, pieces=(), kind=jnp.bfloat16):
    result = scale * jax.random.normal(stream_key, extent, jnp.float32)
    if pieces:
        result = result * steps_of(stream_key, extent, pieces, -0.22, 0.18)
    return jnp.clip(result, -reach, reach).astype(kind)


def setup_inputs(seed: int = 0) -> dict:
    splits = jax.random.split(jax.random.key(seed), 5)
    return {
        "cotangent": gaussian(splits[0], (FIELDS, LEV, NX, NY), 1.0, 6.0, ((1, 4), (2, 8)), jnp.float32),
        "blocks": draw_blocks(jax.random.fold_in(splits[4], 71), 0),
        "couple": draw_couple(jax.random.fold_in(splits[4], 71), 0),
        "kappa": jnp.clip(0.05 + 0.19 * jax.random.uniform(splits[3], (NX, NY), jnp.float32) ** steps_of(splits[3], (NX, NY), ((0, 8),), -0.2, 0.2), 0.05, 0.24),
    }


def reference(cotangent, blocks, couple, kappa):
    fields = cotangent.shape[0]
    segment_parts = LEV // PIECE
    columns = NX * NY
    shaped = cotangent.reshape(fields, segment_parts, PIECE, columns).transpose(1, 0, 2, 3)
    matrices = blocks.reshape(fields, segment_parts, PIECE, PIECE).transpose(1, 0, 2, 3)
    retain = couple.reshape(fields, segment_parts, columns).transpose(1, 0, 2)

    def descend(carried, inputs):
        piece_cot, matrix, retain_piece = inputs
        forced = piece_cot.at[:, -1, :].add(carried)
        adjoint = jnp.einsum("fkl,fkc->flc", matrix, forced, precision=lax.Precision.HIGHEST)
        totals = jnp.sum(piece_cot, axis=1)
        return retain_piece * (totals + carried), adjoint

    start = jnp.zeros((fields, columns), jnp.float32)
    final_carry, layered_pile = lax.scan(descend, start, (shaped, matrices, retain), reverse=True)
    section = layered_pile.transpose(1, 0, 2, 3).reshape(fields, LEV, NX, NY)
    weighted = kappa * section
    padded = jnp.pad(weighted, ((0, 0), (0, 0), (1, 1), (1, 1)))
    cross_strip_span = padded[:, :, 2:, 1:-1] + padded[:, :, :-2, 1:-1]
    along_strip = padded[:, :, 1:-1, 2:] + padded[:, :, 1:-1, :-2]
    return section + cross_strip_span + along_strip - 4.0 * weighted
```

```python
import functools

import jax
import jax.numpy as jnp
from jax import lax
from jax.experimental import pallas as pl
from jax.experimental.pallas import tpu as pltpu
from jax.sharding import PartitionSpec as P

VMEM = pl.BlockSpec(memory_space=pltpu.VMEM)
LIMIT = 16 * 1024 * 1024


def call(body, outs, cost, *args):
    return pl.pallas_call(
        body,
        out_shape=outs,
        in_specs=[VMEM] * len(args),
        out_specs=[VMEM] * len(outs),
        compiler_params=pltpu.CompilerParams(vmem_limit_bytes=LIMIT),
        cost_estimate=pl.CostEstimate(flops=cost[0], bytes_accessed=cost[1], transcendentals=0),
    )(*args)


def f32(*shape):
    return jax.ShapeDtypeStruct(shape, jnp.float32)


def halves(x):
    high = x.astype(jnp.bfloat16)
    low = (x - high.astype(jnp.float32)).astype(jnp.bfloat16)
    return high, low


def product(high, low, x):
    a, b = halves(x)
    dot = functools.partial(jnp.dot, preferred_element_type=jnp.float32)
    return dot(high, a) + (dot(high, b) + dot(low, a))


def pack_kernel(dims, cot, couple, kappa, first, second, pair):
    fields, levels, rows = dims
    even = lax.rem(lax.axis_index("strip"), 2) == 0
    for f in range(fields):
        base = f * levels * rows
        low = kappa[0:1, :] * cot[pl.ds(base, levels, stride=rows), :]
        high = kappa[rows - 1 : rows, :] * cot[pl.ds(base + rows - 1, levels, stride=rows), :]
        first[f * levels : (f + 1) * levels, :] = jnp.where(even, high, low)
        second[f * levels : (f + 1) * levels, :] = jnp.where(even, low, high)
        block = cot[base : base + levels * rows, :].reshape(levels, rows, -1)
        weight = couple[f * rows : (f + 1) * rows, :]
        pair[f * rows : (f + 1) * rows, :] = weight * jnp.sum(block, axis=0)
        pair[(fields + f) * rows : (fields + f + 1) * rows, :] = weight


def across(weighted):
    lane = lax.broadcasted_iota(jnp.int32, weighted.shape, 1)
    last = weighted.shape[1] - 1
    left = jnp.where(lane == 0, 0.0, pltpu.roll(weighted, 1, 1))
    right = jnp.where(lane == last, 0.0, pltpu.roll(weighted, last, 1))
    return left + right


def main_kernel(dims, cot, blocks, kappa, out, high_ref, low_ref):
    fields, levels, rows = dims
    for f in range(fields):
        high, low = halves(jnp.transpose(blocks[f]))
        high_ref[f], low_ref[f] = high, low
        base = f * levels * rows
        load = lambda x: cot[pl.ds(base + x, levels, stride=rows), :]
        scaled = lambda x, v: v * kappa[x : x + 1, :]
        before = None
        here = load(0)
        here_w = scaled(0, here)
        for x in range(rows):
            total = here - 4.0 * here_w + across(here_w)
            if before is not None:
                total = total + before
            if x + 1 < rows:
                after = load(x + 1)
                after_w = scaled(x + 1, after)
                total = total + after_w
            out[pl.ds(base + x, levels, stride=rows), :] = product(high, low, total)
            before, here, here_w = here_w, after, after_w


def carry_kernel(dims, count, *refs):
    fields, rows = dims
    kappa = refs[0]
    received = refs[1:count]
    spread, first, second = refs[count:]
    size = fields * rows
    mine = lax.axis_index("lev")
    even = lax.rem(lax.axis_index("strip"), 2) == 0
    carried = jnp.zeros((size, kappa.shape[1]), jnp.float32)
    for piece in range(count - 1, 0, -1):
        offset, weight = received[0][0:size, :], received[0][size:, :]
        for step in range(2, count):
            here = partner(mine, step, count) == piece
            offset = jnp.where(here, received[step - 1][0:size, :], offset)
            weight = jnp.where(here, received[step - 1][size:, :], weight)
        carried = jnp.where(piece > mine, offset + weight * carried, carried)
    tall = jnp.concatenate([kappa[...]] * fields, axis=0)
    weighted = tall * carried
    row = lax.rem(lax.broadcasted_iota(jnp.int32, weighted.shape, 0), rows)
    below = jnp.where(row == 0, 0.0, pltpu.roll(weighted, 1, 0))
    above = jnp.where(row == rows - 1, 0.0, pltpu.roll(weighted, size - 1, 0))
    spread[...] = carried - 4.0 * weighted + across(weighted) + below + above
    first[...] = jnp.zeros_like(first)
    second[...] = jnp.zeros_like(second)
    for f in range(fields):
        low = weighted[f * rows : f * rows + 1, :]
        high = weighted[(f + 1) * rows - 1 : (f + 1) * rows, :]
        first[f : f + 1, :] = jnp.where(even, high, low)
        second[f : f + 1, :] = jnp.where(even, low, high)


def final_kernel(dims, base_out, last, spread, high_ref, low_ref, near, far, near_c, far_c, out):
    fields, levels, rows = dims
    even = lax.rem(lax.axis_index("strip"), 2) == 0
    for f in range(fields):
        base = f * levels * rows
        piece = spread[f * rows : (f + 1) * rows, :]
        for l in range(levels):
            at = base + l * rows
            factor = last[f * levels + l : f * levels + l + 1, :]
            out[at : at + rows, :] = base_out[at : at + rows, :] + factor * piece
        near_f = near[f * levels : (f + 1) * levels, :]
        far_f = far[f * levels : (f + 1) * levels, :]
        top = lax.broadcasted_iota(jnp.int32, near_f.shape, 0) == levels - 1
        near_f = near_f + jnp.where(top, near_c[f : f + 1, :], 0.0)
        far_f = far_f + jnp.where(top, far_c[f : f + 1, :], 0.0)
        low = jnp.where(even, far_f, near_f)
        high = jnp.where(even, near_f, far_f)
        extra = product(high_ref[f], low_ref[f], jnp.concatenate([low, high], axis=1))
        columns = low.shape[1]
        for x, part in ((0, extra[:, :columns]), (rows - 1, extra[:, columns:])):
            at = pl.ds(base + x, levels, stride=rows)
            out[at, :] = out[at, :] + part


def partner(index, step, count):
    if count & (count - 1) == 0:
        return index ^ step
    return lax.rem(index + step, count)


def on_device(cotangent, blocks, couple, kappa):
    fields, levels, rows, columns = cotangent.shape
    pieces, strips = lax.axis_size("lev"), lax.axis_size("strip")
    dims = (fields, levels, rows)
    cot = cotangent.reshape(fields * levels * rows, columns)
    weights = couple.reshape(fields * rows, columns)
    edge = f32(fields * levels, columns)
    nbytes = 4 * cot.size

    first, second, pair = call(
        functools.partial(pack_kernel, dims),
        [edge, edge, f32(2 * fields * rows, columns)],
        (cot.size, nbytes),
        cot,
        weights,
        kappa,
    )
    one = [(i, i ^ 1) for i in range(strips) if i ^ 1 < strips]
    two = [(i, j) for i in range(strips) for j in [((i + 1) ^ 1) - 1] if 0 <= j < strips]
    near = lax.ppermute(first, "strip", one)
    far = lax.ppermute(second, "strip", two)
    received = []
    for step in range(1, pieces):
        if pieces & (pieces - 1) == 0:
            pairs = [(i, i ^ step) for i in range(pieces)]
        else:
            pairs = [((i + step) % pieces, i) for i in range(pieces)]
        received.append(lax.ppermute(pair, "lev", pairs))
    base_out, high, low = call(
        functools.partial(main_kernel, dims),
        [f32(*cot.shape)] + [jax.ShapeDtypeStruct((fields, levels, levels), jnp.bfloat16)] * 2,
        (6 * levels * cot.size, 2 * nbytes),
        cot,
        blocks,
        kappa,
    )
    tiny = f32(-(-fields // 8) * 8, columns)
    spread, first_c, second_c = call(
        functools.partial(carry_kernel, (fields, rows), pieces),
        [f32(fields * rows, columns), tiny, tiny],
        (weights.size * 10, weights.size * 32),
        kappa,
        *received,
    )
    near_c = lax.ppermute(first_c, "strip", one)
    far_c = lax.ppermute(second_c, "strip", two)
    last = jnp.broadcast_to(blocks[:, levels - 1, :].reshape(fields * levels, 1), (fields * levels, columns))
    (out,) = call(
        functools.partial(final_kernel, dims),
        [f32(*cot.shape)],
        (4 * cot.size, 2 * nbytes),
        base_out,
        last,
        spread,
        high,
        low,
        near,
        far,
        near_c,
        far_c,
    )
    return out.reshape(cotangent.shape)


def solution(mesh):
    placed = (
        P(None, "lev", "strip", None),
        P(None, "lev", None),
        P(None, "lev", "strip", None),
        P("strip", None),
    )
    return jax.shard_map(
        on_device,
        mesh=mesh,
        in_specs=placed,
        out_specs=P(None, "lev", "strip", None),
        check_vma=False,
    )
```

```python
import functools

import jax
import jax.numpy as jnp
from jax import lax
from jax.experimental import pallas as pl
from jax.experimental.pallas import tpu as pltpu
from jax.sharding import PartitionSpec as P

VMEM = pl.BlockSpec(memory_space=pltpu.VMEM)
HBM = pl.BlockSpec(memory_space=pltpu.HBM)
LIMIT = 16 * 1024 * 1024


def call(body, outs, cost, *args, ins=None, out_specs=None, scratch=()):
    return pl.pallas_call(
        body,
        out_shape=outs,
        in_specs=ins or [VMEM] * len(args),
        out_specs=out_specs or [VMEM] * len(outs),
        scratch_shapes=list(scratch),
        compiler_params=pltpu.CompilerParams(vmem_limit_bytes=LIMIT),
        cost_estimate=pl.CostEstimate(flops=cost[0], bytes_accessed=cost[1], transcendentals=0),
    )(*args)


def f32(*shape):
    return jax.ShapeDtypeStruct(shape, jnp.float32)


def halves(x):
    high = x.astype(jnp.bfloat16)
    low = (x - high.astype(jnp.float32)).astype(jnp.bfloat16)
    return high, low


def product(high, low, x):
    a, b = halves(x)
    dot = functools.partial(jnp.dot, preferred_element_type=jnp.float32)
    return dot(high, a) + (dot(high, b) + dot(low, a))


def even_strip():
    return lax.rem(lax.axis_index("strip"), 2) == 0


def pack_kernel(
    dims, cot_hbm, couple_hbm, kappa_hbm, cot, kappa, first, second, pair, couple, sems
):
    fields, levels, rows = dims
    chunk = levels * rows
    small = [
        pltpu.make_async_copy(kappa_hbm, kappa, sems.at[fields]),
        pltpu.make_async_copy(couple_hbm, couple, sems.at[fields + 1]),
    ]
    large = [
        pltpu.make_async_copy(
            cot_hbm.at[pl.ds(f * chunk, chunk)], cot.at[pl.ds(f * chunk, chunk)], sems.at[f]
        )
        for f in range(fields)
    ]
    for copy in small + large:
        copy.start()
    for copy in small:
        copy.wait()
    even = even_strip()
    for f in range(fields):
        large[f].wait()
        base = f * chunk
        low = kappa[0:1, :] * cot[pl.ds(base, levels, stride=rows), :]
        high = kappa[rows - 1 : rows, :] * cot[pl.ds(base + rows - 1, levels, stride=rows), :]
        first[f * levels : (f + 1) * levels, :] = jnp.where(even, high, low)
        second[f * levels : (f + 1) * levels, :] = jnp.where(even, low, high)
        block = cot[base : base + chunk, :].reshape(levels, rows, -1)
        weight = couple[f * rows : (f + 1) * rows, :]
        pair[f * rows : (f + 1) * rows, :] = weight * jnp.sum(block, axis=0)
        pair[(fields + f) * rows : (fields + f + 1) * rows, :] = weight


def chip_pair(mine, own, other, size):
    bottom = lax.rem(mine, 2) == 0
    offset = (own[0:size, :], other[0:size, :])
    weight = (own[size:, :], other[size:, :])
    order = lambda v: (jnp.where(bottom, v[0], v[1]), jnp.where(bottom, v[1], v[0]))
    return order(offset), order(weight)


def compose_kernel(own, other, chip):
    size = own.shape[0] // 2
    offset, weight = chip_pair(lax.axis_index("lev"), own, other, size)
    chip[0:size, :] = offset[0] + weight[0] * offset[1]
    if chip.shape[0] > size:
        chip[size:, :] = weight[0] * weight[1]


def across(weighted):
    lane = lax.broadcasted_iota(jnp.int32, weighted.shape, 1)
    last = weighted.shape[1] - 1
    left = jnp.where(lane == 0, 0.0, pltpu.roll(weighted, 1, 1))
    right = jnp.where(lane == last, 0.0, pltpu.roll(weighted, last, 1))
    return left + right


def carry_kernel(dims, chips, kappa, own, other, *refs):
    fields, _, rows = dims
    received = refs[: chips - 1]
    spread, first, second = refs[chips - 1 :]
    size = fields * rows
    mine = lax.axis_index("lev")
    my_chip = lax.div(mine, 2)
    offset, weight = chip_pair(mine, own, other, size)
    entry = jnp.zeros((size, kappa.shape[1]), jnp.float32)
    for chip in range(chips - 1, 0, -1):
        value, factor = received[0][0:size, :], received[0][size:, :] if chips > 2 else None
        for step in range(2, chips):
            here = partner(my_chip, step, chips) == chip
            value = jnp.where(here, received[step - 1][0:size, :], value)
            factor = jnp.where(here, received[step - 1][size:, :], factor)
        longer = value if chip == chips - 1 else value + factor * entry
        entry = jnp.where(chip > my_chip, longer, entry)
    carried = jnp.where(lax.rem(mine, 2) == 0, offset[1] + weight[1] * entry, entry)
    weighted = jnp.concatenate([kappa[...]] * fields, axis=0) * carried
    row = lax.rem(lax.broadcasted_iota(jnp.int32, weighted.shape, 0), rows)
    below = jnp.where(row == 0, 0.0, pltpu.roll(weighted, 1, 0))
    above = jnp.where(row == rows - 1, 0.0, pltpu.roll(weighted, size - 1, 0))
    spread[...] = carried - 4.0 * weighted + across(weighted) + below + above
    first[...] = jnp.zeros_like(first)
    second[...] = jnp.zeros_like(second)
    even = even_strip()
    for f in range(fields):
        low = weighted[f * rows : f * rows + 1, :]
        high = weighted[(f + 1) * rows - 1 : (f + 1) * rows, :]
        first[f : f + 1, :] = jnp.where(even, high, low)
        second[f : f + 1, :] = jnp.where(even, low, high)


def main_kernel(dims, cot, blocks, kappa, spread, out, high_ref, low_ref):
    fields, levels, rows = dims
    top = lax.broadcasted_iota(jnp.int32, (levels, kappa.shape[1]), 0) == levels - 1
    for f in range(fields):
        high, low = halves(jnp.transpose(blocks[f]))
        high_ref[f], low_ref[f] = high, low
        base = f * levels * rows
        load = lambda x: cot[pl.ds(base + x, levels, stride=rows), :]
        scaled = lambda x, v: v * kappa[x : x + 1, :]
        before = None
        here = load(0)
        here_w = scaled(0, here)
        for x in range(rows):
            total = here - 4.0 * here_w + across(here_w)
            if before is not None:
                total = total + before
            if x + 1 < rows:
                after = load(x + 1)
                after_w = scaled(x + 1, after)
                total = total + after_w
            total = total + jnp.where(top, spread[f * rows + x : f * rows + x + 1, :], 0.0)
            out[pl.ds(base + x, levels, stride=rows), :] = product(high, low, total)
            before, here, here_w = here_w, after, after_w


def final_kernel(dims, strips, base_out, high, low, near, far, near_c, far_c, out_hbm, out, sems):
    fields, levels, rows = dims
    chunk = levels * rows
    columns = near.shape[1]
    mine = lax.axis_index("strip")
    even = even_strip()
    has_near = jnp.logical_or(jnp.logical_not(even), mine + 1 < strips)
    has_far = jnp.where(even, mine > 0, mine + 1 < strips)
    top = lax.broadcasted_iota(jnp.int32, (levels, columns), 0) == levels - 1
    copies = []
    for f in range(fields):
        base = f * chunk
        out[base : base + chunk, :] = base_out[base : base + chunk, :]
        sides = []
        for here, halo, halo_c in ((has_near, near, near_c), (has_far, far, far_c)):
            value = halo[f * levels : (f + 1) * levels, :]
            value = value + jnp.where(top, halo_c[f : f + 1, :], 0.0)
            sides.append(jnp.where(here, value, 0.0))
        below = jnp.where(even, sides[1], sides[0])
        above = jnp.where(even, sides[0], sides[1])
        extra = product(high[f], low[f], jnp.concatenate([below, above], axis=1))
        for x, part in ((0, extra[:, :columns]), (rows - 1, extra[:, columns:])):
            at = pl.ds(base + x, levels, stride=rows)
            out[at, :] = out[at, :] + part
        span = pl.ds(base, chunk)
        copies.append(pltpu.make_async_copy(out.at[span], out_hbm.at[span], sems.at[f]))
        copies[-1].start()
    for copy in copies:
        copy.wait()


def partner(index, step, count):
    if count & (count - 1) == 0:
        return index ^ step
    return lax.rem(index + step, count)


def sources(step, count):
    if count & (count - 1) == 0:
        return [i ^ step for i in range(count)]
    return [(i + step) % count for i in range(count)]


def swaps(strips, pieces, shift):
    pairs = []
    for strip in range(strips):
        other = ((strip + shift) ^ 1) - shift
        for piece in range(pieces):
            mine = strip * pieces + piece
            inside = 0 <= other < strips
            pairs.append((mine, other * pieces + piece if inside else mine ^ 1))
    return pairs


def compute(cotangent, blocks, couple, kappa):
    fields, levels, rows, columns = cotangent.shape
    pieces, strips = lax.axis_size("lev"), lax.axis_size("strip")
    chips = pieces // 2
    dims = (fields, levels, rows)
    cot = cotangent.reshape(fields * levels * rows, columns)
    size = fields * rows
    edge = f32(fields * levels, columns)
    nbytes = 4 * cot.size
    square = jax.ShapeDtypeStruct((fields, levels, levels), jnp.bfloat16)
    tiny = f32(-(-fields // 8) * 8, columns)
    whole = ("strip", "lev")
    one, two = swaps(strips, pieces, 0), swaps(strips, pieces, 1)

    cot, kappa, first, second, pair = call(
        functools.partial(pack_kernel, dims),
        [f32(*cot.shape), f32(rows, columns), edge, edge, f32(2 * size, columns)],
        (cot.size, nbytes),
        *(
            pltpu.with_memory_space_constraint(x, pltpu.HBM)
            for x in (cot, couple.reshape(size, columns), kappa)
        ),
        ins=[HBM] * 3,
        scratch=[pltpu.VMEM((size, columns), jnp.float32), pltpu.SemaphoreType.DMA((fields + 2,))],
    )
    other = lax.ppermute(pair, "lev", [(i, i ^ 1) for i in range(pieces)])
    near = lax.ppermute(first, whole, one)
    (chip,) = call(
        compose_kernel, [f32(size * (2 if chips > 2 else 1), columns)], (4 * size, 16 * size), pair, other
    )
    received = []
    for step in range(1, chips):
        moves = [(2 * s + c, 2 * i + c) for i, s in enumerate(sources(step, chips)) for c in range(2)]
        received.append(lax.ppermute(chip, "lev", moves))
    far = lax.ppermute(second, whole, two)
    spread, first, second = call(
        functools.partial(carry_kernel, dims, chips),
        [f32(size, columns), tiny, tiny],
        (size * columns * 10, size * columns * 32),
        kappa,
        pair,
        other,
        *received,
    )
    far_c = lax.ppermute(second, whole, two)
    near_c = lax.ppermute(first, whole, one)
    base_out, high, low = call(
        functools.partial(main_kernel, dims),
        [f32(*cot.shape), square, square],
        (6 * levels * cot.size, 2 * nbytes),
        cot,
        blocks,
        kappa,
        spread,
    )
    (out,) = call(
        functools.partial(final_kernel, dims, strips),
        [f32(*cot.shape)],
        (4 * cot.size, 2 * nbytes),
        base_out,
        high,
        low,
        near,
        far,
        near_c,
        far_c,
        out_specs=[HBM],
        scratch=[pltpu.VMEM(cot.shape, jnp.float32), pltpu.SemaphoreType.DMA((fields,))],
    )
    return out.reshape(cotangent.shape)


def solution(mesh):
    placed = (
        P(None, "lev", "strip", None),
        P(None, "lev", None),
        P(None, "lev", "strip", None),
        P("strip", None),
    )
    return jax.shard_map(
        compute,
        mesh=mesh,
        in_specs=placed,
        out_specs=P(None, "lev", "strip", None),
        check_vma=False,
    )
```

```python
import functools

import jax
import jax.numpy as jnp
from jax import lax
from jax.experimental import pallas as pl
from jax.experimental.pallas import tpu as pltpu
from jax.sharding import PartitionSpec as P

VMEM = pl.BlockSpec(memory_space=pltpu.VMEM)
HBM = pl.BlockSpec(memory_space=pltpu.HBM)
LIMIT = 16 * 1024 * 1024


def call(body, outs, cost, *args, ins=None, out_specs=None, scratch=()):
    return pl.pallas_call(
        body,
        out_shape=outs,
        in_specs=ins or [VMEM] * len(args),
        out_specs=out_specs or [VMEM] * len(outs),
        scratch_shapes=list(scratch),
        compiler_params=pltpu.CompilerParams(vmem_limit_bytes=LIMIT),
        cost_estimate=pl.CostEstimate(flops=cost[0], bytes_accessed=cost[1], transcendentals=0),
    )(*args)


def f32(*shape):
    return jax.ShapeDtypeStruct(shape, jnp.float32)


def halves(x):
    high = x.astype(jnp.bfloat16)
    low = (x - high.astype(jnp.float32)).astype(jnp.bfloat16)
    return high, low


def product(matrix, x):
    high, low = halves(x)
    stacked = jnp.concatenate([high, low, high], axis=0)
    return jnp.dot(matrix, stacked, preferred_element_type=jnp.float32)


def even_strip():
    return lax.rem(lax.axis_index("strip"), 2) == 0


def pack_kernel(
    dims, cot_hbm, couple_hbm, kappa_hbm, cot, kappa, first, second, pair, couple, sems
):
    fields, levels, rows = dims
    chunk = levels * rows
    small = [
        pltpu.make_async_copy(kappa_hbm, kappa, sems.at[fields]),
        pltpu.make_async_copy(couple_hbm, couple, sems.at[fields + 1]),
    ]
    large = [
        pltpu.make_async_copy(
            cot_hbm.at[pl.ds(f * chunk, chunk)], cot.at[pl.ds(f * chunk, chunk)], sems.at[f]
        )
        for f in range(fields)
    ]
    for copy in small + large:
        copy.start()
    for copy in small:
        copy.wait()
    even = even_strip()
    for f in range(fields):
        large[f].wait()
        base = f * chunk
        low = kappa[0:1, :] * cot[pl.ds(base, levels, stride=rows), :]
        high = kappa[rows - 1 : rows, :] * cot[pl.ds(base + rows - 1, levels, stride=rows), :]
        first[f * levels : (f + 1) * levels, :] = jnp.where(even, high, low)
        second[f * levels : (f + 1) * levels, :] = jnp.where(even, low, high)
        block = cot[base : base + chunk, :].reshape(levels, rows, -1)
        weight = couple[f * rows : (f + 1) * rows, :]
        pair[f * rows : (f + 1) * rows, :] = weight * jnp.sum(block, axis=0)
        pair[(fields + f) * rows : (fields + f + 1) * rows, :] = weight


def chip_pair(mine, own, other, size):
    bottom = lax.rem(mine, 2) == 0
    offset = (own[0:size, :], other[0:size, :])
    weight = (own[size:, :], other[size:, :])
    order = lambda v: (jnp.where(bottom, v[0], v[1]), jnp.where(bottom, v[1], v[0]))
    return order(offset), order(weight)


def compose_kernel(own, other, chip):
    size = own.shape[0] // 2
    offset, weight = chip_pair(lax.axis_index("lev"), own, other, size)
    chip[0:size, :] = offset[0] + weight[0] * offset[1]
    if chip.shape[0] > size:
        chip[size:, :] = weight[0] * weight[1]


def across(weighted):
    lane = lax.broadcasted_iota(jnp.int32, weighted.shape, 1)
    last = weighted.shape[1] - 1
    left = jnp.where(lane == 0, 0.0, pltpu.roll(weighted, 1, 1))
    right = jnp.where(lane == last, 0.0, pltpu.roll(weighted, last, 1))
    return left + right


def carry_kernel(dims, chips, kappa, own, other, *refs):
    fields, _, rows = dims
    received = refs[: chips - 1]
    spread, first, second = refs[chips - 1 :]
    size = fields * rows
    mine = lax.axis_index("lev")
    my_chip = lax.div(mine, 2)
    offset, weight = chip_pair(mine, own, other, size)
    entry = jnp.zeros((size, kappa.shape[1]), jnp.float32)
    for chip in range(chips - 1, 0, -1):
        value, factor = received[0][0:size, :], received[0][size:, :] if chips > 2 else None
        for step in range(2, chips):
            here = partner(my_chip, step, chips) == chip
            value = jnp.where(here, received[step - 1][0:size, :], value)
            factor = jnp.where(here, received[step - 1][size:, :], factor)
        longer = value if chip == chips - 1 else value + factor * entry
        entry = jnp.where(chip > my_chip, longer, entry)
    carried = jnp.where(lax.rem(mine, 2) == 0, offset[1] + weight[1] * entry, entry)
    weighted = jnp.concatenate([kappa[...]] * fields, axis=0) * carried
    row = lax.rem(lax.broadcasted_iota(jnp.int32, weighted.shape, 0), rows)
    below = jnp.where(row == 0, 0.0, pltpu.roll(weighted, 1, 0))
    above = jnp.where(row == rows - 1, 0.0, pltpu.roll(weighted, size - 1, 0))
    spread[...] = carried - 4.0 * weighted + across(weighted) + below + above
    first[...] = jnp.zeros_like(first)
    second[...] = jnp.zeros_like(second)
    even = even_strip()
    for f in range(fields):
        low = weighted[f * rows : f * rows + 1, :]
        high = weighted[(f + 1) * rows - 1 : (f + 1) * rows, :]
        first[f : f + 1, :] = jnp.where(even, high, low)
        second[f : f + 1, :] = jnp.where(even, low, high)


def main_kernel(dims, cot, blocks, kappa, spread, out, matrices):
    fields, levels, rows = dims
    columns = kappa.shape[1]
    top = lax.broadcasted_iota(jnp.int32, (levels, columns), 0) == levels - 1
    for f in range(fields):
        high, low = halves(jnp.transpose(blocks[f]))
        matrix = jnp.concatenate([high, high, low], axis=1)
        matrices[f] = matrix
        base = f * levels * rows
        at = lambda x: pl.ds(base + x, levels, stride=rows)
        before, here = None, cot[at(0), :]
        here_w = here * kappa[0:1, :]
        totals = []
        for x in range(rows):
            total = here - 4.0 * here_w + across(here_w)
            if before is not None:
                total = total + before
            before = here_w
            if x + 1 < rows:
                here = cot[at(x + 1), :]
                here_w = here * kappa[x + 1 : x + 2, :]
                total = total + here_w
            totals.append(total + jnp.where(top, spread[f * rows + x : f * rows + x + 1, :], 0.0))
            if len(totals) == 2 or x + 1 == rows:
                result = product(matrix, jnp.concatenate(totals, axis=1))
                for i in range(len(totals)):
                    start = x + 1 - len(totals) + i
                    out[at(start), :] = result[:, i * columns : (i + 1) * columns]
                totals = []


def final_kernel(dims, strips, base_out, matrices, near, far, near_c, far_c, out_hbm, out, sems):
    fields, levels, rows = dims
    chunk = levels * rows
    columns = near.shape[1]
    mine = lax.axis_index("strip")
    even = even_strip()
    has_near = jnp.logical_or(jnp.logical_not(even), mine + 1 < strips)
    has_far = jnp.where(even, mine > 0, mine + 1 < strips)
    top = lax.broadcasted_iota(jnp.int32, (levels, columns), 0) == levels - 1
    copies = []
    for f in range(fields):
        base = f * chunk
        out[base : base + chunk, :] = base_out[base : base + chunk, :]
        sides = []
        for here, halo, halo_c in ((has_near, near, near_c), (has_far, far, far_c)):
            value = halo[f * levels : (f + 1) * levels, :]
            value = value + jnp.where(top, halo_c[f : f + 1, :], 0.0)
            sides.append(jnp.where(here, value, 0.0))
        below = jnp.where(even, sides[1], sides[0])
        above = jnp.where(even, sides[0], sides[1])
        extra = product(matrices[f], jnp.concatenate([below, above], axis=1))
        for x, part in ((0, extra[:, :columns]), (rows - 1, extra[:, columns:])):
            at = pl.ds(base + x, levels, stride=rows)
            out[at, :] = out[at, :] + part
        span = pl.ds(base, chunk)
        copies.append(pltpu.make_async_copy(out.at[span], out_hbm.at[span], sems.at[f]))
        copies[-1].start()
    for copy in copies:
        copy.wait()


def partner(index, step, count):
    if count & (count - 1) == 0:
        return index ^ step
    return lax.rem(index + step, count)


def sources(step, count):
    if count & (count - 1) == 0:
        return [i ^ step for i in range(count)]
    return [(i + step) % count for i in range(count)]


def swaps(strips, pieces, shift):
    pairs = []
    for strip in range(strips):
        other = ((strip + shift) ^ 1) - shift
        for piece in range(pieces):
            mine = strip * pieces + piece
            inside = 0 <= other < strips
            pairs.append((mine, other * pieces + piece if inside else mine ^ 1))
    return pairs


def compute(cotangent, blocks, couple, kappa):
    fields, levels, rows, columns = cotangent.shape
    pieces, strips = lax.axis_size("lev"), lax.axis_size("strip")
    chips = pieces // 2
    dims = (fields, levels, rows)
    cot = cotangent.reshape(fields * levels * rows, columns)
    size = fields * rows
    edge = f32(fields * levels, columns)
    nbytes = 4 * cot.size
    wide = jax.ShapeDtypeStruct((fields, levels, 3 * levels), jnp.bfloat16)
    tiny = f32(-(-fields // 8) * 8, columns)
    whole = ("strip", "lev")
    one, two = swaps(strips, pieces, 0), swaps(strips, pieces, 1)

    cot, kappa, first, second, pair = call(
        functools.partial(pack_kernel, dims),
        [f32(*cot.shape), f32(rows, columns), edge, edge, f32(2 * size, columns)],
        (cot.size, nbytes),
        *(
            pltpu.with_memory_space_constraint(x, pltpu.HBM)
            for x in (cot, couple.reshape(size, columns), kappa)
        ),
        ins=[HBM] * 3,
        scratch=[pltpu.VMEM((size, columns), jnp.float32), pltpu.SemaphoreType.DMA((fields + 2,))],
    )
    other = lax.ppermute(pair, "lev", [(i, i ^ 1) for i in range(pieces)])
    near = lax.ppermute(first, whole, one)
    (chip,) = call(
        compose_kernel, [f32(size * (2 if chips > 2 else 1), columns)], (4 * size, 16 * size), pair, other
    )
    received = []
    for step in range(1, chips):
        moves = [(2 * s + c, 2 * i + c) for i, s in enumerate(sources(step, chips)) for c in range(2)]
        received.append(lax.ppermute(chip, "lev", moves))
    far = lax.ppermute(second, whole, two)
    spread, first, second = call(
        functools.partial(carry_kernel, dims, chips),
        [f32(size, columns), tiny, tiny],
        (size * columns * 10, size * columns * 32),
        kappa,
        pair,
        other,
        *received,
    )
    far_c = lax.ppermute(second, whole, two)
    near_c = lax.ppermute(first, whole, one)
    base_out, matrices = call(
        functools.partial(main_kernel, dims),
        [f32(*cot.shape), wide],
        (6 * levels * cot.size, 2 * nbytes),
        cot,
        blocks,
        kappa,
        spread,
    )
    (out,) = call(
        functools.partial(final_kernel, dims, strips),
        [f32(*cot.shape)],
        (4 * cot.size, 2 * nbytes),
        base_out,
        matrices,
        near,
        far,
        near_c,
        far_c,
        out_specs=[HBM],
        scratch=[pltpu.VMEM(cot.shape, jnp.float32), pltpu.SemaphoreType.DMA((fields,))],
    )
    return out.reshape(cotangent.shape)


def solution(mesh):
    placed = (
        P(None, "lev", "strip", None),
        P(None, "lev", None),
        P(None, "lev", "strip", None),
        P("strip", None),
    )
    return jax.shard_map(
        compute,
        mesh=mesh,
        in_specs=placed,
        out_specs=P(None, "lev", "strip", None),
        check_vma=False,
    )
```

```python
import functools

import jax
import jax.numpy as jnp
from jax import lax
from jax.experimental import pallas as pl
from jax.experimental.pallas import tpu as pltpu
from jax.sharding import PartitionSpec as P

VMEM = pl.BlockSpec(memory_space=pltpu.VMEM)
HBM = pl.BlockSpec(memory_space=pltpu.HBM)
LIMIT = 16 * 1024 * 1024
LATE = 1


def call(body, outs, cost, *args, ins=None, out_specs=None, scratch=(), aliases=None):
    return pl.pallas_call(
        body,
        out_shape=outs,
        in_specs=ins or [VMEM] * len(args),
        out_specs=out_specs or [VMEM] * len(outs),
        scratch_shapes=list(scratch),
        input_output_aliases=aliases or {},
        compiler_params=pltpu.CompilerParams(vmem_limit_bytes=LIMIT),
        cost_estimate=pl.CostEstimate(flops=cost[0], bytes_accessed=cost[1], transcendentals=0),
    )(*args)


def f32(*shape):
    return jax.ShapeDtypeStruct(shape, jnp.float32)


def halves(x):
    high = x.astype(jnp.bfloat16)
    low = (x - high.astype(jnp.float32)).astype(jnp.bfloat16)
    return high, low


def product(matrix, x):
    high, low = halves(x)
    stacked = jnp.concatenate([high, low, high], axis=0)
    return jnp.dot(matrix, stacked, preferred_element_type=jnp.float32)


def first_is_above():
    return lax.rem(lax.axis_index("strip"), 2) == 0


def pack_kernel(
    dims, cot_hbm, couple_hbm, kappa_hbm, cot, kappa, first, second, pair, couple, sems
):
    fields, levels, rows = dims
    chunk = levels * rows
    small = [
        pltpu.make_async_copy(kappa_hbm, kappa, sems.at[fields]),
        pltpu.make_async_copy(couple_hbm, couple, sems.at[fields + 1]),
    ]
    large = [
        pltpu.make_async_copy(
            cot_hbm.at[pl.ds(f * chunk, chunk)], cot.at[pl.ds(f * chunk, chunk)], sems.at[f]
        )
        for f in range(fields)
    ]
    for copy in small + large:
        copy.start()
    for copy in small:
        copy.wait()
    size = fields * rows
    pair[size:, :] = couple[...]
    is_above = first_is_above()
    for f in range(fields):
        large[f].wait()
        base = f * chunk
        low = kappa[0:1, :] * cot[pl.ds(base, levels, stride=rows), :]
        high = kappa[rows - 1 : rows, :] * cot[pl.ds(base + rows - 1, levels, stride=rows), :]
        first[f * levels : (f + 1) * levels, :] = jnp.where(is_above, high, low)
        second[f * levels : (f + 1) * levels, :] = jnp.where(is_above, low, high)
        mine = slice(f * rows, (f + 1) * rows)
        block = cot[base : base + chunk, :].reshape(levels, rows, -1)
        pair[mine, :] = couple[mine, :] * jnp.sum(block, axis=0)


def chip_pair(mine, own, other, size):
    bottom = lax.rem(mine, 2) == 0
    offset = (own[0:size, :], other[0:size, :])
    weight = (own[size:, :], other[size:, :])
    order = lambda v: (jnp.where(bottom, v[0], v[1]), jnp.where(bottom, v[1], v[0]))
    return order(offset), order(weight)


def compose_kernel(own, other, chip):
    size = own.shape[0] // 2
    offset, weight = chip_pair(lax.axis_index("lev"), own, other, size)
    chip[0:size, :] = offset[0] + weight[0] * offset[1]
    if chip.shape[0] > size:
        chip[size:, :] = weight[0] * weight[1]


def across(weighted):
    lane = lax.broadcasted_iota(jnp.int32, weighted.shape, 1)
    last = weighted.shape[1] - 1
    left = jnp.where(lane == 0, 0.0, pltpu.roll(weighted, 1, 1))
    right = jnp.where(lane == last, 0.0, pltpu.roll(weighted, last, 1))
    return left + right


def carry_kernel(dims, chips, kappa, own, other, *refs):
    fields, _, rows = dims
    received = refs[: chips - 1]
    spread, first, second = refs[chips - 1 :]
    size = fields * rows
    mine = lax.axis_index("lev")
    my_chip = lax.div(mine, 2)
    offset, weight = chip_pair(mine, own, other, size)
    entry = jnp.zeros((size, kappa.shape[1]), jnp.float32)
    for chip in range(chips - 1, 0, -1):
        value, factor = received[0][0:size, :], received[0][size:, :] if chips > 2 else None
        for step in range(2, chips):
            here = partner(my_chip, step, chips) == chip
            value = jnp.where(here, received[step - 1][0:size, :], value)
            factor = jnp.where(here, received[step - 1][size:, :], factor)
        longer = value if chip == chips - 1 else value + factor * entry
        entry = jnp.where(chip > my_chip, longer, entry)
    carried = jnp.where(lax.rem(mine, 2) == 0, offset[1] + weight[1] * entry, entry)
    weighted = jnp.concatenate([kappa[...]] * fields, axis=0) * carried
    row = lax.rem(lax.broadcasted_iota(jnp.int32, weighted.shape, 0), rows)
    below = jnp.where(row == 0, 0.0, pltpu.roll(weighted, 1, 0))
    above = jnp.where(row == rows - 1, 0.0, pltpu.roll(weighted, size - 1, 0))
    spread[...] = carried - 4.0 * weighted + across(weighted) + below + above
    first[...] = jnp.zeros_like(first)
    second[...] = jnp.zeros_like(second)
    is_above = first_is_above()
    for f in range(fields):
        low = weighted[f * rows : f * rows + 1, :]
        high = weighted[(f + 1) * rows - 1 : (f + 1) * rows, :]
        first[f : f + 1, :] = jnp.where(is_above, high, low)
        second[f : f + 1, :] = jnp.where(is_above, low, high)


def writes(dims, stage, out, sems, late):
    fields, levels, rows = dims
    split = (fields - LATE) * levels
    part = pl.ds(split, LATE * levels) if late else pl.ds(0, split)
    return [
        pltpu.make_async_copy(stage.at[x, part], out.at[part, x, 0], sems.at[x])
        for x in range(1, rows - 1)
        if LATE or not late
    ]


def main_kernel(dims, cot, blocks, kappa, spread, out, stage, matrices, sems):
    fields, levels, rows = dims
    columns = kappa.shape[1]
    top = lax.broadcasted_iota(jnp.int32, (8, columns), 0) == 7
    copies = writes(dims, stage, out, sems, False)
    for f in range(fields):
        high, low = halves(jnp.transpose(blocks[f]))
        matrix = jnp.concatenate([high, high, low], axis=1)
        matrices[f] = matrix
        load = lambda x: cot[pl.ds(f * levels * rows + x, levels, stride=rows), :]
        before, here = None, load(0)
        here_w = here * kappa[0:1, :]
        totals = []
        for x in range(rows):
            total = here * (1.0 - 4.0 * kappa[x : x + 1, :]) + across(here_w)
            if before is not None:
                total = total + before
            before = here_w
            if x + 1 < rows:
                here = load(x + 1)
                here_w = here * kappa[x + 1 : x + 2, :]
                total = total + here_w
            carry = jnp.where(top, spread[f * rows + x : f * rows + x + 1, :], 0.0)
            total = jnp.concatenate([total[: levels - 8], total[levels - 8 :] + carry], axis=0)
            totals.append(total)
            if len(totals) < 2 and x + 1 < rows:
                continue
            result = product(matrix, jnp.concatenate(totals, axis=1))
            for i in range(len(totals)):
                row = x + 1 - len(totals) + i
                stage[row, f * levels : (f + 1) * levels] = result[:, i * columns : (i + 1) * columns]
            totals = []
        if f + 1 == fields - LATE:
            for copy in copies:
                copy.start()
    for copy in copies:
        copy.wait()


def final_kernel(
    dims, strips, started, stage, matrices, first, second, first_c, second_c, out, edges, sems
):
    fields, levels, rows = dims
    columns = first.shape[1]
    copies = writes(dims, stage, out, sems, True)
    for copy in copies:
        copy.start()
    mine = lax.axis_index("strip")
    is_above = first_is_above()
    below_exists, above_exists = mine > 0, mine + 1 < strips
    top = lax.broadcasted_iota(jnp.int32, (8, columns), 0) == 7
    for f in range(fields):
        at = slice(f * levels, (f + 1) * levels)
        sides = []
        for halo, halo_c in ((first, first_c), (second, second_c)):
            carry = jnp.where(top, halo_c[f : f + 1, :], 0.0)
            value = halo[at, :]
            sides.append(
                jnp.concatenate([value[: levels - 8], value[levels - 8 :] + carry], axis=0)
            )
        below = jnp.where(below_exists, jnp.where(is_above, sides[1], sides[0]), 0.0)
        above = jnp.where(above_exists, jnp.where(is_above, sides[0], sides[1]), 0.0)
        extra = product(matrices[f], jnp.concatenate([below, above], axis=1))
        for side, x in ((0, 0), (1, rows - 1)):
            edges[side, at] = stage[x, at] + extra[:, side * columns : (side + 1) * columns]
    for side, x in ((0, 0), (1, rows - 1)):
        copies.append(pltpu.make_async_copy(edges.at[side], out.at[:, x, 0], sems.at[x]))
        copies[-1].start()
    for copy in copies:
        copy.wait()


def partner(index, step, count):
    if count & (count - 1) == 0:
        return index ^ step
    return lax.rem(index + step, count)


def sources(step, count):
    if count & (count - 1) == 0:
        return [i ^ step for i in range(count)]
    return [(i + step) % count for i in range(count)]


def swaps(strips, pieces, turn):
    pairs = []
    for strip in range(strips):
        other = ((strip + turn) ^ 1) - turn
        for piece in range(pieces):
            mine = strip * pieces + piece
            inside = 0 <= other < strips
            pairs.append((mine, other * pieces + piece if inside else mine ^ 1))
    return pairs


def compute(cotangent, blocks, couple, kappa):
    fields, levels, rows, columns = cotangent.shape
    pieces, strips = lax.axis_size("lev"), lax.axis_size("strip")
    chips = pieces // 2
    dims = (fields, levels, rows)
    cot = cotangent.reshape(fields * levels * rows, columns)
    rowwise = f32(fields * levels, rows, 1, columns)
    by_row = f32(rows, fields * levels, columns)
    size = fields * rows
    edge = f32(fields * levels, columns)
    nbytes = 4 * cot.size
    wide = jax.ShapeDtypeStruct((fields, levels, 3 * levels), jnp.bfloat16)
    tiny = f32(-(-fields // 8) * 8, columns)
    whole = ("strip", "lev")
    one, two = swaps(strips, pieces, 0), swaps(strips, pieces, 1)

    held, kappa, first, second, pair = call(
        functools.partial(pack_kernel, dims),
        [f32(*cot.shape), f32(rows, columns), edge, edge, f32(2 * size, columns)],
        (cot.size, nbytes),
        *(
            pltpu.with_memory_space_constraint(x, pltpu.HBM)
            for x in (cot, couple.reshape(size, columns), kappa)
        ),
        ins=[HBM] * 3,
        scratch=[pltpu.VMEM((size, columns), jnp.float32), pltpu.SemaphoreType.DMA((fields + 2,))],
    )
    other = lax.ppermute(pair, "lev", [(i, i ^ 1) for i in range(pieces)])
    near = lax.ppermute(first, whole, one)
    (chip,) = call(
        compose_kernel, [f32(size * (2 if chips > 2 else 1), columns)], (4 * size, 16 * size), pair, other
    )
    received = []
    for step in range(1, chips):
        moves = [(2 * s + c, 2 * i + c) for i, s in enumerate(sources(step, chips)) for c in range(2)]
        received.append(lax.ppermute(chip, "lev", moves))
    far = lax.ppermute(second, whole, two)
    spread, first, second = call(
        functools.partial(carry_kernel, dims, chips),
        [f32(size, columns), tiny, tiny],
        (size * columns * 10, size * columns * 32),
        kappa,
        pair,
        other,
        *received,
    )
    far_c = lax.ppermute(second, whole, two)
    near_c = lax.ppermute(first, whole, one)
    started, stage, matrices = call(
        functools.partial(main_kernel, dims),
        [rowwise, by_row, wide],
        (6 * levels * cot.size, 2 * nbytes),
        held,
        blocks,
        kappa,
        spread,
        out_specs=[HBM, VMEM, VMEM],
        scratch=[pltpu.SemaphoreType.DMA((rows,))],
    )
    (out,) = call(
        functools.partial(final_kernel, dims, strips),
        [rowwise],
        (cot.size, nbytes // 4),
        started,
        stage,
        matrices,
        near,
        far,
        near_c,
        far_c,
        ins=[HBM] + [VMEM] * 6,
        out_specs=[HBM],
        scratch=[
            pltpu.VMEM((2, fields * levels, columns), jnp.float32),
            pltpu.SemaphoreType.DMA((rows,)),
        ],
        aliases={0: 0},
    )
    return out.reshape(cotangent.shape)


def solution(mesh):
    placed = (
        P(None, "lev", "strip", None),
        P(None, "lev", None),
        P(None, "lev", "strip", None),
        P("strip", None),
    )
    return jax.shard_map(
        compute,
        mesh=mesh,
        in_specs=placed,
        out_specs=P(None, "lev", "strip", None),
        check_vma=False,
    )
```

```python
import functools

import jax
import jax.numpy as jnp
from jax import lax
from jax.experimental import pallas as pl
from jax.experimental.pallas import tpu as pltpu
from jax.sharding import PartitionSpec as P

VMEM = pl.BlockSpec(memory_space=pltpu.VMEM)
HBM = pl.BlockSpec(memory_space=pltpu.HBM)
LIMIT = 16 * 1024 * 1024
AHEAD = 1
LATE = 0


def call(body, outs, cost, *args, ins=None, out_specs=None, scratch=(), aliases=None):
    return pl.pallas_call(
        body,
        out_shape=outs,
        in_specs=ins or [VMEM] * len(args),
        out_specs=out_specs or [VMEM] * len(outs),
        scratch_shapes=list(scratch),
        input_output_aliases=aliases or {},
        compiler_params=pltpu.CompilerParams(vmem_limit_bytes=LIMIT),
        cost_estimate=pl.CostEstimate(flops=cost[0], bytes_accessed=cost[1], transcendentals=0),
    )(*args)


def f32(*shape):
    return jax.ShapeDtypeStruct(shape, jnp.float32)


def halves(x):
    high = x.astype(jnp.bfloat16)
    low = (x - high.astype(jnp.float32)).astype(jnp.bfloat16)
    return high, low


def product(matrix, x):
    high, low = halves(x)
    stacked = jnp.concatenate([high, low, high], axis=0)
    return jnp.dot(matrix, stacked, preferred_element_type=jnp.float32)


def first_is_above():
    return lax.rem(lax.axis_index("strip"), 2) == 0


def pack_kernel(
    dims, cot_hbm, couple_hbm, kappa_hbm, cot, kappa, first, second, pair, couple, sems
):
    fields, levels, rows = dims
    chunk = levels * rows
    small = [
        pltpu.make_async_copy(kappa_hbm, kappa, sems.at[fields]),
        pltpu.make_async_copy(couple_hbm, couple, sems.at[fields + 1]),
    ]
    large = [
        pltpu.make_async_copy(
            cot_hbm.at[pl.ds(f * chunk, chunk)], cot.at[pl.ds(f * chunk, chunk)], sems.at[f]
        )
        for f in range(fields)
    ]
    for copy in small + large:
        copy.start()
    for copy in small:
        copy.wait()
    size = fields * rows
    pair[size:, :] = couple[...]
    is_above = first_is_above()
    for f in range(fields):
        large[f].wait()
        base = f * chunk
        low = kappa[0:1, :] * cot[pl.ds(base, levels, stride=rows), :]
        high = kappa[rows - 1 : rows, :] * cot[pl.ds(base + rows - 1, levels, stride=rows), :]
        first[f * levels : (f + 1) * levels, :] = jnp.where(is_above, high, low)
        second[f * levels : (f + 1) * levels, :] = jnp.where(is_above, low, high)
        mine = slice(f * rows, (f + 1) * rows)
        block = cot[base : base + chunk, :].reshape(levels, rows, -1)
        pair[mine, :] = couple[mine, :] * jnp.sum(block, axis=0)


def chip_pair(mine, own, other, size):
    bottom = lax.rem(mine, 2) == 0
    offset = (own[0:size, :], other[0:size, :])
    weight = (own[size:, :], other[size:, :])
    order = lambda v: (jnp.where(bottom, v[0], v[1]), jnp.where(bottom, v[1], v[0]))
    return order(offset), order(weight)


def compose_kernel(own, other, chip):
    size = own.shape[0] // 2
    offset, weight = chip_pair(lax.axis_index("lev"), own, other, size)
    chip[0:size, :] = offset[0] + weight[0] * offset[1]
    if chip.shape[0] > size:
        chip[size:, :] = weight[0] * weight[1]


def across(weighted):
    lane = lax.broadcasted_iota(jnp.int32, weighted.shape, 1)
    last = weighted.shape[1] - 1
    left = jnp.where(lane == 0, 0.0, pltpu.roll(weighted, 1, 1))
    right = jnp.where(lane == last, 0.0, pltpu.roll(weighted, last, 1))
    return left + right


def carry_kernel(dims, chips, kappa, own, other, *refs):
    fields, _, rows = dims
    received = refs[: chips - 1]
    spread, first, second = refs[chips - 1 :]
    size = fields * rows
    mine = lax.axis_index("lev")
    my_chip = lax.div(mine, 2)
    offset, weight = chip_pair(mine, own, other, size)
    entry = jnp.zeros((size, kappa.shape[1]), jnp.float32)
    for chip in range(chips - 1, 0, -1):
        value, factor = received[0][0:size, :], received[0][size:, :] if chips > 2 else None
        for step in range(2, chips):
            here = partner(my_chip, step, chips) == chip
            value = jnp.where(here, received[step - 1][0:size, :], value)
            factor = jnp.where(here, received[step - 1][size:, :], factor)
        longer = value if chip == chips - 1 else value + factor * entry
        entry = jnp.where(chip > my_chip, longer, entry)
    carried = jnp.where(lax.rem(mine, 2) == 0, offset[1] + weight[1] * entry, entry)
    weighted = jnp.concatenate([kappa[...]] * fields, axis=0) * carried
    row = lax.rem(lax.broadcasted_iota(jnp.int32, weighted.shape, 0), rows)
    below = jnp.where(row == 0, 0.0, pltpu.roll(weighted, 1, 0))
    above = jnp.where(row == rows - 1, 0.0, pltpu.roll(weighted, size - 1, 0))
    spread[...] = carried - 4.0 * weighted + across(weighted) + below + above
    first[...] = jnp.zeros_like(first)
    second[...] = jnp.zeros_like(second)
    is_above = first_is_above()
    for f in range(fields):
        low = weighted[f * rows : f * rows + 1, :]
        high = weighted[(f + 1) * rows - 1 : (f + 1) * rows, :]
        first[f : f + 1, :] = jnp.where(is_above, high, low)
        second[f : f + 1, :] = jnp.where(is_above, low, high)


def writes(dims, chosen, stage, out, sem):
    _, levels, rows = dims
    part = pl.ds(chosen.start * levels, len(chosen) * levels)
    for x in range(1, rows - 1):
        pltpu.make_async_copy(stage.at[x, part], out.at[part, x, 0], sem).start()
    inner = stage.at[pl.ds(1, rows - 2), part]
    return pltpu.make_async_copy(inner, inner, sem)


def groups(fields):
    late = range(fields - LATE, fields)
    return range(AHEAD), range(AHEAD, fields - 1), range(fields - 1, late.start), late


def section(dims, f, matrix, cot, kappa, spread, store):
    levels, rows = dims[1:]
    columns = kappa.shape[1]
    load = lambda x: cot[pl.ds(f * levels * rows + x, levels, stride=rows), :]
    top = lax.broadcasted_iota(jnp.int32, (8, columns), 0) == 7
    before, here = None, load(0)
    here_w = here * kappa[0:1, :]
    totals = []
    for x in range(rows):
        total = here * (1.0 - 4.0 * kappa[x : x + 1, :]) + across(here_w)
        if before is not None:
            total = total + before
        before = here_w
        if x + 1 < rows:
            here = load(x + 1)
            here_w = here * kappa[x + 1 : x + 2, :]
            total = total + here_w
        if spread is not None:
            carry = jnp.where(top, spread[f * rows + x : f * rows + x + 1, :], 0.0)
            total = jnp.concatenate([total[: levels - 8], total[levels - 8 :] + carry], axis=0)
        totals.append(total)
        if len(totals) < 2 and x + 1 < rows:
            continue
        result = product(matrix, jnp.concatenate(totals, axis=1))
        for i in range(len(totals)):
            store(x + 1 - len(totals) + i, result[:, i * columns : (i + 1) * columns])
        totals = []


def matrix_of(turned):
    high, low = halves(turned)
    return jnp.concatenate([high, high, low], axis=1)


def ahead_kernel(dims, cot, blocks, kappa, stage):
    levels = dims[1]
    for f in range(AHEAD):

        def store(x, value):
            stage[x, f * levels : (f + 1) * levels] = value

        section(dims, f, matrix_of(jnp.transpose(blocks[f])), cot, kappa, None, store)


def main_kernel(dims, cot, blocks, kappa, spread, ahead, out, stage, matrices, last, sems):
    fields, levels, rows = dims
    columns = kappa.shape[1]
    copies = []
    for f in range(fields):
        own = slice(f * levels, (f + 1) * levels)
        turned = jnp.transpose(blocks[f])
        last[own, :] = jnp.broadcast_to(turned[:, levels - 1 :], (levels, columns))
        matrix = matrix_of(turned)
        matrices[f] = matrix
        if f < AHEAD:
            for x in range(rows):
                carry = spread[f * rows + x : f * rows + x + 1, :]
                stage[x, own] = ahead[x, own] + last[own, :] * carry
        else:

            def store(x, value):
                stage[x, own] = value

            section(dims, f, matrix, cot, kappa, spread, store)
        for i, group in enumerate(groups(fields)[:3]):
            if f + 1 == group.stop and len(group):
                copies.append(writes(dims, group, stage, out, sems.at[i]))
    for copy in copies:
        copy.wait()


def halo_kernel(dims, strips, stage, matrices, first, second, edges):
    fields, levels, rows = dims
    columns = first.shape[1]
    mine = lax.axis_index("strip")
    is_above = first_is_above()
    first_exists = jnp.where(is_above, mine + 1 < strips, mine > 0)
    second_exists = jnp.where(is_above, mine > 0, mine + 1 < strips)
    for f in range(fields):
        at = slice(f * levels, (f + 1) * levels)
        one = jnp.where(first_exists, first[at, :], 0.0)
        two = jnp.where(second_exists, second[at, :], 0.0)
        below = jnp.where(is_above, two, one)
        above = jnp.where(is_above, one, two)
        extra = product(matrices[f], jnp.concatenate([below, above], axis=1))
        for side, x in ((0, 0), (1, rows - 1)):
            edges[side, at] = stage[x, at] + extra[:, side * columns : (side + 1) * columns]


def final_kernel(
    dims, strips, started, stage, partial, last, first, second, out, edges, sems
):
    fields, levels, rows = dims
    mine = lax.axis_index("strip")
    is_above = first_is_above()
    below_exists, above_exists = mine > 0, mine + 1 < strips
    late = groups(fields)[3]
    copies = [writes(dims, late, stage, out, sems.at[2])] if len(late) else []
    for side, x in ((0, 0), (1, rows - 1)):
        for f in range(fields):
            row = slice(f, f + 1)
            one, two = first[row, :], second[row, :]
            below = jnp.where(below_exists, jnp.where(is_above, two, one), 0.0)
            above = jnp.where(above_exists, jnp.where(is_above, one, two), 0.0)
            at = slice(f * levels, (f + 1) * levels)
            edges[side, at] = partial[side, at] + last[at, :] * (above if side else below)
        copies.append(pltpu.make_async_copy(edges.at[side], out.at[:, x, 0], sems.at[side]))
        copies[-1].start()
    for copy in copies:
        copy.wait()


def partner(index, step, count):
    if count & (count - 1) == 0:
        return index ^ step
    return lax.rem(index + step, count)


def sources(step, count):
    if count & (count - 1) == 0:
        return [i ^ step for i in range(count)]
    return [(i + step) % count for i in range(count)]


def swaps(strips, pieces, turn):
    pairs = []
    for strip in range(strips):
        other = ((strip + turn) ^ 1) - turn
        for piece in range(pieces):
            mine = strip * pieces + piece
            inside = 0 <= other < strips
            pairs.append((mine, other * pieces + piece if inside else mine ^ 1))
    return pairs


def compute(cotangent, blocks, couple, kappa):
    fields, levels, rows, columns = cotangent.shape
    pieces, strips = lax.axis_size("lev"), lax.axis_size("strip")
    chips = pieces // 2
    dims = (fields, levels, rows)
    cot = cotangent.reshape(fields * levels * rows, columns)
    rowwise = f32(fields * levels, rows, 1, columns)
    by_row = f32(rows, fields * levels, columns)
    size = fields * rows
    edge = f32(fields * levels, columns)
    nbytes = 4 * cot.size
    wide = jax.ShapeDtypeStruct((fields, levels, 3 * levels), jnp.bfloat16)
    tiny = f32(-(-fields // 8) * 8, columns)
    whole = ("strip", "lev")
    one, two = swaps(strips, pieces, 0), swaps(strips, pieces, 1)

    held, kappa, first, second, pair = call(
        functools.partial(pack_kernel, dims),
        [f32(*cot.shape), f32(rows, columns), edge, edge, f32(2 * size, columns)],
        (cot.size, nbytes),
        *(
            pltpu.with_memory_space_constraint(x, pltpu.HBM)
            for x in (cot, couple.reshape(size, columns), kappa)
        ),
        ins=[HBM] * 3,
        scratch=[pltpu.VMEM((size, columns), jnp.float32), pltpu.SemaphoreType.DMA((fields + 2,))],
    )
    other = lax.ppermute(pair, "lev", [(i, i ^ 1) for i in range(pieces)])
    near = lax.ppermute(first, whole, one)
    (chip,) = call(
        compose_kernel, [f32(size * (2 if chips > 2 else 1), columns)], (4 * size, 16 * size), pair, other
    )
    received = []
    for step in range(1, chips):
        moves = [(2 * s + c, 2 * i + c) for i, s in enumerate(sources(step, chips)) for c in range(2)]
        received.append(lax.ppermute(chip, "lev", moves))
    far = lax.ppermute(second, whole, two)
    (ahead,) = call(
        functools.partial(ahead_kernel, dims),
        [f32(rows, AHEAD * levels, columns)],
        (6 * levels * cot.size * AHEAD // fields, 2 * nbytes * AHEAD // fields),
        held,
        blocks,
        kappa,
    )
    spread, first, second = call(
        functools.partial(carry_kernel, dims, chips),
        [f32(size, columns), tiny, tiny],
        (size * columns * 10, size * columns * 32),
        kappa,
        pair,
        other,
        *received,
    )
    far_c = lax.ppermute(second, whole, two)
    near_c = lax.ppermute(first, whole, one)
    started, stage, matrices, last = call(
        functools.partial(main_kernel, dims),
        [rowwise, by_row, wide, edge],
        (6 * levels * cot.size, 2 * nbytes),
        held,
        blocks,
        kappa,
        spread,
        ahead,
        out_specs=[HBM, VMEM, VMEM, VMEM],
        scratch=[pltpu.SemaphoreType.DMA((3,))],
    )
    sides = f32(2, fields * levels, columns)
    (partial,) = call(
        functools.partial(halo_kernel, dims, strips),
        [sides],
        (12 * levels * edge.size, 16 * edge.size),
        stage,
        matrices,
        near,
        far,
    )
    (out,) = call(
        functools.partial(final_kernel, dims, strips),
        [rowwise],
        (4 * edge.size, 16 * edge.size),
        started,
        stage,
        partial,
        last,
        near_c,
        far_c,
        ins=[HBM] + [VMEM] * 5,
        out_specs=[HBM],
        scratch=[
            pltpu.VMEM(sides.shape, jnp.float32),
            pltpu.SemaphoreType.DMA((3,)),
        ],
        aliases={0: 0},
    )
    return out.reshape(cotangent.shape)


def solution(mesh):
    placed = (
        P(None, "lev", "strip", None),
        P(None, "lev", None),
        P(None, "lev", "strip", None),
        P("strip", None),
    )
    return jax.shard_map(
        compute,
        mesh=mesh,
        in_specs=placed,
        out_specs=P(None, "lev", "strip", None),
        check_vma=False,
    )
```

```python
import functools

import jax
import jax.numpy as jnp
from jax import lax
from jax.experimental import pallas as pl
from jax.experimental.pallas import tpu as pltpu
from jax.sharding import PartitionSpec as P

VMEM = pl.BlockSpec(memory_space=pltpu.VMEM)
HBM = pl.BlockSpec(memory_space=pltpu.HBM)
LIMIT = 16 * 1024 * 1024
AHEAD = (1, 2, 3)


def call(body, outs, cost, *args, ins=None, out_specs=None, scratch=(), aliases=None):
    return pl.pallas_call(
        body,
        out_shape=outs,
        in_specs=ins or [VMEM] * len(args),
        out_specs=out_specs or [VMEM] * len(outs),
        scratch_shapes=list(scratch),
        input_output_aliases=aliases or {},
        compiler_params=pltpu.CompilerParams(vmem_limit_bytes=LIMIT),
        cost_estimate=pl.CostEstimate(flops=cost[0], bytes_accessed=cost[1], transcendentals=0),
    )(*args)


def f32(*shape):
    return jax.ShapeDtypeStruct(shape, jnp.float32)


def halves(x):
    high = x.astype(jnp.bfloat16)
    low = (x - high.astype(jnp.float32)).astype(jnp.bfloat16)
    return high, low


def product(matrix, x):
    high, low = halves(x)
    stacked = jnp.concatenate([high, low, high], axis=0)
    return jnp.dot(matrix, stacked, preferred_element_type=jnp.float32)


def first_is_above():
    return lax.rem(lax.axis_index("strip"), 2) == 0


def pack_kernel(
    dims, cot_hbm, couple_hbm, kappa_hbm, cot, kappa, first, second, pair, couple, sems
):
    fields, levels, rows = dims
    chunk = levels * rows
    small = [
        pltpu.make_async_copy(kappa_hbm, kappa, sems.at[fields]),
        pltpu.make_async_copy(couple_hbm, couple, sems.at[fields + 1]),
    ]
    large = [
        pltpu.make_async_copy(
            cot_hbm.at[pl.ds(f * chunk, chunk)], cot.at[pl.ds(f * chunk, chunk)], sems.at[f]
        )
        for f in range(fields)
    ]
    for copy in small + large:
        copy.start()
    for copy in small:
        copy.wait()
    size = fields * rows
    pair[size:, :] = couple[...]
    is_above = first_is_above()
    for f in range(fields):
        large[f].wait()
        base = f * chunk
        low = kappa[0:1, :] * cot[pl.ds(base, levels, stride=rows), :]
        high = kappa[rows - 1 : rows, :] * cot[pl.ds(base + rows - 1, levels, stride=rows), :]
        first[f * levels : (f + 1) * levels, :] = jnp.where(is_above, high, low)
        second[f * levels : (f + 1) * levels, :] = jnp.where(is_above, low, high)
        mine = slice(f * rows, (f + 1) * rows)
        block = cot[base : base + chunk, :].reshape(levels, rows, -1)
        pair[mine, :] = couple[mine, :] * jnp.sum(block, axis=0)


def chip_pair(mine, own, other, size):
    bottom = lax.rem(mine, 2) == 0
    offset = (own[0:size, :], other[0:size, :])
    weight = (own[size:, :], other[size:, :])
    order = lambda v: (jnp.where(bottom, v[0], v[1]), jnp.where(bottom, v[1], v[0]))
    return order(offset), order(weight)


def compose_kernel(own, other, chip):
    size = own.shape[0] // 2
    offset, weight = chip_pair(lax.axis_index("lev"), own, other, size)
    chip[0:size, :] = offset[0] + weight[0] * offset[1]
    if chip.shape[0] > size:
        chip[size:, :] = weight[0] * weight[1]


def across(weighted):
    lane = lax.broadcasted_iota(jnp.int32, weighted.shape, 1)
    last = weighted.shape[1] - 1
    left = jnp.where(lane == 0, 0.0, pltpu.roll(weighted, 1, 1))
    right = jnp.where(lane == last, 0.0, pltpu.roll(weighted, last, 1))
    return left + right


def carry_kernel(dims, chips, kappa, own, other, *refs):
    fields, _, rows = dims
    received = refs[: chips - 1]
    spread, first, second = refs[chips - 1 :]
    size = fields * rows
    mine = lax.axis_index("lev")
    my_chip = lax.div(mine, 2)
    offset, weight = chip_pair(mine, own, other, size)
    entry = jnp.zeros((size, kappa.shape[1]), jnp.float32)
    for chip in range(chips - 1, 0, -1):
        value, factor = received[0][0:size, :], received[0][size:, :] if chips > 2 else None
        for step in range(2, chips):
            here = partner(my_chip, step, chips) == chip
            value = jnp.where(here, received[step - 1][0:size, :], value)
            factor = jnp.where(here, received[step - 1][size:, :], factor)
        longer = value if chip == chips - 1 else value + factor * entry
        entry = jnp.where(chip > my_chip, longer, entry)
    carried = jnp.where(lax.rem(mine, 2) == 0, offset[1] + weight[1] * entry, entry)
    weighted = jnp.concatenate([kappa[...]] * fields, axis=0) * carried
    row = lax.rem(lax.broadcasted_iota(jnp.int32, weighted.shape, 0), rows)
    below = jnp.where(row == 0, 0.0, pltpu.roll(weighted, 1, 0))
    above = jnp.where(row == rows - 1, 0.0, pltpu.roll(weighted, size - 1, 0))
    spread[...] = carried - 4.0 * weighted + across(weighted) + below + above
    first[...] = jnp.zeros_like(first)
    second[...] = jnp.zeros_like(second)
    is_above = first_is_above()
    for f in range(fields):
        low = weighted[f * rows : f * rows + 1, :]
        high = weighted[(f + 1) * rows - 1 : (f + 1) * rows, :]
        first[f : f + 1, :] = jnp.where(is_above, high, low)
        second[f : f + 1, :] = jnp.where(is_above, low, high)


def writes(dims, chosen, stage, out, sem):
    levels, rows = dims[1:]
    part = pl.ds(chosen.start * levels, len(chosen) * levels)
    for x in range(1, rows - 1):
        pltpu.make_async_copy(stage.at[x, part], out.at[part, x, 0], sem).start()


def landed(dims, chosen, stage):
    levels, rows = dims[1:]
    return stage.at[pl.ds(1, rows - 2), pl.ds(chosen.start * levels, len(chosen) * levels)]


def groups(fields):
    return range(1), range(1, fields - 1), range(fields - 1, fields)


def section(dims, f, matrix, cot, kappa, spread, store):
    levels, rows = dims[1:]
    columns = kappa.shape[1]
    load = lambda x: cot[pl.ds(f * levels * rows + x, levels, stride=rows), :]
    top = lax.broadcasted_iota(jnp.int32, (8, columns), 0) == 7
    before, here = None, load(0)
    here_w = here * kappa[0:1, :]
    totals = []
    for x in range(rows):
        total = here * (1.0 - 4.0 * kappa[x : x + 1, :]) + across(here_w)
        if before is not None:
            total = total + before
        before = here_w
        if x + 1 < rows:
            here = load(x + 1)
            here_w = here * kappa[x + 1 : x + 2, :]
            total = total + here_w
        if spread is not None:
            carry = jnp.where(top, spread[f * rows + x : f * rows + x + 1, :], 0.0)
            total = jnp.concatenate([total[: levels - 8], total[levels - 8 :] + carry], axis=0)
        totals.append(total)
        if len(totals) < 2 and x + 1 < rows:
            continue
        result = product(matrix, jnp.concatenate(totals, axis=1))
        for i in range(len(totals)):
            store(x + 1 - len(totals) + i, result[:, i * columns : (i + 1) * columns])
        totals = []


def matrix_of(turned):
    high, low = halves(turned)
    return jnp.concatenate([high, high, low], axis=1)


def strip_kinds():
    strip = lax.axis_index("strip")
    odd = lax.rem(strip, 2) == 1
    return odd, jnp.logical_and(jnp.logical_not(odd), strip > 0), strip == 0


def ahead_kernel(dims, cot, blocks, kappa, stage):
    fields, levels = dims[:2]

    def run(chosen):
        for f in chosen:

            def store(x, value):
                stage[x, f * levels : (f + 1) * levels] = value

            section(dims, f, matrix_of(jnp.transpose(blocks[f])), cot, kappa, None, store)

    run(range(AHEAD[0]))
    for kind, count in list(zip(strip_kinds(), AHEAD))[1:]:
        pl.when(kind)(functools.partial(run, range(AHEAD[0], min(count, fields))))


def main_kernel(dims, cot, blocks, kappa, spread, ahead, out, stage, matrices, last, sems):
    fields, levels, rows = dims
    columns = kappa.shape[1]

    def run(done):
        for f in range(fields):
            own = slice(f * levels, (f + 1) * levels)
            turned = jnp.transpose(blocks[f])
            last[own, :] = jnp.broadcast_to(turned[:, levels - 1 :], (levels, columns))
            matrix = matrix_of(turned)
            matrices[f] = matrix
            if f < done:
                for x in range(rows):
                    carry = spread[f * rows + x : f * rows + x + 1, :]
                    stage[x, own] = ahead[x, own] + last[own, :] * carry
            else:

                def store(x, value):
                    stage[x, own] = value

                section(dims, f, matrix, cot, kappa, spread, store)
            for i, group in enumerate(groups(fields)):
                if f + 1 == group.stop and len(group):
                    writes(dims, group, stage, out, sems.at[i])

    for kind, count in zip(strip_kinds(), AHEAD):
        pl.when(kind)(functools.partial(run, min(count, fields)))
    for i, group in enumerate(groups(fields)):
        if len(group):
            inner = landed(dims, group, stage)
            pltpu.make_async_copy(inner, inner, sems.at[i]).wait()


def halo_kernel(dims, strips, stage, matrices, first, second, edges):
    fields, levels, rows = dims
    columns = first.shape[1]
    mine = lax.axis_index("strip")
    is_above = first_is_above()
    first_exists = jnp.where(is_above, mine + 1 < strips, mine > 0)
    second_exists = jnp.where(is_above, mine > 0, mine + 1 < strips)
    for f in range(fields):
        at = slice(f * levels, (f + 1) * levels)
        one = jnp.where(first_exists, first[at, :], 0.0)
        two = jnp.where(second_exists, second[at, :], 0.0)
        below = jnp.where(is_above, two, one)
        above = jnp.where(is_above, one, two)
        extra = product(matrices[f], jnp.concatenate([below, above], axis=1))
        for side, x in ((0, 0), (1, rows - 1)):
            edges[side, at] = stage[x, at] + extra[:, side * columns : (side + 1) * columns]


def final_kernel(dims, strips, started, partial, last, first, inner, second, out, edges, sems):
    fields, levels, rows = dims
    mine = lax.axis_index("strip")
    is_above = first_is_above()
    below_exists, above_exists = mine > 0, mine + 1 < strips
    copies = []
    for side, x in ((0, 0), (1, rows - 1)):
        for f in range(fields):
            row = slice(f, f + 1)
            one, two = jnp.where(mine < 2, first[row, :], inner[row, :]), second[row, :]
            below = jnp.where(below_exists, jnp.where(is_above, two, one), 0.0)
            above = jnp.where(above_exists, jnp.where(is_above, one, two), 0.0)
            at = slice(f * levels, (f + 1) * levels)
            edges[side, at] = partial[side, at] + last[at, :] * (above if side else below)
        copies.append(pltpu.make_async_copy(edges.at[side], out.at[:, x, 0], sems.at[side]))
        copies[-1].start()
    for copy in copies:
        copy.wait()


def partner(index, step, count):
    if count & (count - 1) == 0:
        return index ^ step
    return lax.rem(index + step, count)


def sources(step, count):
    if count & (count - 1) == 0:
        return [i ^ step for i in range(count)]
    return [(i + step) % count for i in range(count)]


def swaps(strips, pieces, turn, chosen=None):
    pairs = []
    for strip in range(strips):
        other = ((strip + turn) ^ 1) - turn
        for piece in range(pieces):
            mine = strip * pieces + piece
            inside = 0 <= other < strips
            inside = inside and strip in (chosen or range(strips))
            pairs.append((mine, other * pieces + piece if inside else mine ^ 1))
    return pairs


def compute(cotangent, blocks, couple, kappa):
    fields, levels, rows, columns = cotangent.shape
    pieces, strips = lax.axis_size("lev"), lax.axis_size("strip")
    chips = pieces // 2
    dims = (fields, levels, rows)
    cot = cotangent.reshape(fields * levels * rows, columns)
    rowwise = f32(fields * levels, rows, 1, columns)
    by_row = f32(rows, fields * levels, columns)
    size = fields * rows
    edge = f32(fields * levels, columns)
    nbytes = 4 * cot.size
    wide = jax.ShapeDtypeStruct((fields, levels, 3 * levels), jnp.bfloat16)
    tiny = f32(-(-fields // 8) * 8, columns)
    whole = ("strip", "lev")
    one, two = swaps(strips, pieces, 0), swaps(strips, pieces, 1)

    held, kappa, first, second, pair = call(
        functools.partial(pack_kernel, dims),
        [f32(*cot.shape), f32(rows, columns), edge, edge, f32(2 * size, columns)],
        (cot.size, nbytes),
        *(
            pltpu.with_memory_space_constraint(x, pltpu.HBM)
            for x in (cot, couple.reshape(size, columns), kappa)
        ),
        ins=[HBM] * 3,
        scratch=[pltpu.VMEM((size, columns), jnp.float32), pltpu.SemaphoreType.DMA((fields + 2,))],
    )
    other = lax.ppermute(pair, "lev", [(i, i ^ 1) for i in range(pieces)])
    near = lax.ppermute(first, whole, one)
    (chip,) = call(
        compose_kernel, [f32(size * (2 if chips > 2 else 1), columns)], (4 * size, 16 * size), pair, other
    )
    received = []
    for step in range(1, chips):
        moves = [(2 * s + c, 2 * i + c) for i, s in enumerate(sources(step, chips)) for c in range(2)]
        received.append(lax.ppermute(chip, "lev", moves))
    far = lax.ppermute(second, whole, two)
    (ahead,) = call(
        functools.partial(ahead_kernel, dims),
        [f32(rows, min(AHEAD[-1], fields) * levels, columns)],
        (6 * levels * cot.size * AHEAD[0] // fields, 2 * nbytes * AHEAD[0] // fields),
        held,
        blocks,
        kappa,
    )
    spread, first, second = call(
        functools.partial(carry_kernel, dims, chips),
        [f32(size, columns), tiny, tiny],
        (size * columns * 10, size * columns * 32),
        kappa,
        pair,
        other,
        *received,
    )
    far_c = lax.ppermute(second, whole, two)
    near_c = lax.ppermute(first, whole, swaps(strips, pieces, 0, range(2)))
    inner_c = lax.ppermute(first, whole, swaps(strips, pieces, 0, range(2, strips)))
    started, stage, matrices, last = call(
        functools.partial(main_kernel, dims),
        [rowwise, by_row, wide, edge],
        (6 * levels * cot.size, 2 * nbytes),
        held,
        blocks,
        kappa,
        spread,
        ahead,
        out_specs=[HBM, VMEM, VMEM, VMEM],
        scratch=[pltpu.SemaphoreType.DMA((3,))],
    )
    sides = f32(2, fields * levels, columns)
    (partial,) = call(
        functools.partial(halo_kernel, dims, strips),
        [sides],
        (12 * levels * edge.size, 16 * edge.size),
        stage,
        matrices,
        near,
        far,
    )
    (out,) = call(
        functools.partial(final_kernel, dims, strips),
        [rowwise],
        (4 * edge.size, 16 * edge.size),
        started,
        partial,
        last,
        near_c,
        inner_c,
        far_c,
        ins=[HBM] + [VMEM] * 5,
        out_specs=[HBM],
        scratch=[
            pltpu.VMEM(sides.shape, jnp.float32),
            pltpu.SemaphoreType.DMA((2,)),
        ],
        aliases={0: 0},
    )
    return out.reshape(cotangent.shape)


def solution(mesh):
    placed = (
        P(None, "lev", "strip", None),
        P(None, "lev", None),
        P(None, "lev", "strip", None),
        P("strip", None),
    )
    return jax.shard_map(
        compute,
        mesh=mesh,
        in_specs=placed,
        out_specs=P(None, "lev", "strip", None),
        check_vma=False,
    )
```
